256 devices in a mesh: dp: 16 (over z_hi, y, core), seq: 16 (over x, z_lo).
Axes of the slice: x: 4, y: 4, z: 8 (z_hi: 2, z_lo: 4; z = z_hi * 4 + z_lo), core: 2. Of those that a mesh axis runs over, the one named last changes fastest.
Arguments:
- inputs: bfloat16 [2, 65536, 2048], P(None, 'seq', 'dp'), may hold values from -6 to 6
- cotangent: bfloat16 [2, 65536, 2048], P(None, 'seq', 'dp'), may hold values from -6 to 6
- kernel: bfloat16 [65536, 2048], P('seq', 'dp'), may hold values from -6 to 6
- factor_one: bfloat16 [256, 256], replicated, may hold values from -0.375 to 0.375
- factor_two: bfloat16 [256, 256], replicated, may hold values from -0.375 to 0.375
Outputs:
- grad_inputs: bfloat16 [2, 65536, 2048], P(None, 'seq', 'dp')
- grad_kernel: bfloat16 [65536, 2048], P('seq', 'dp')
- grad_factor_one: float32 [256, 256], replicated
- grad_factor_two: float32 [256, 256], replicated
The draws below stay inside these ranges and needn't reach their ends.
All inputs are finite; a program needn't handle non-finite values.
Results may differ from the reference program's by a relative error of at most 0.0085.
Values may be sent and summed in bfloat16 or wider, within the bound.
A program may use at most 128 MiB of HBM per device.

```python
import math
import jax
import jax.numpy as jnp
from jax import lax

D = 2048
BLOCK = 256
NB = 256
BATCH = 2
SEQ_LEN = 65536


def block_scale(stream_key, extent, split, smallest, high):
    def one(axis_at, blocks):
        steps = jax.random.uniform(jax.random.fold_in(jax.random.fold_in(stream_key, 6), axis_at), (blocks,), jnp.float32, smallest / len(split), high / len(split))
        return jnp.repeat(jnp.exp(steps), extent[axis_at] // blocks).reshape((-1,) + (1,) * (len(extent) - axis_at - 1))

    gain = one(*split[0])
    for cut in split[1:]:
        gain = gain * one(*cut)
    return gain


def normal_values(own_key, shape, spread, limit, pieces=(), kind=jnp.bfloat16):
    drawn = spread * jax.random.normal(own_key, shape, jnp.float32)
    if pieces:
        drawn = drawn * block_scale(own_key, shape, pieces, -0.22, 0.18)
    return jnp.clip(drawn, -limit, limit).astype(kind)


def setup_inputs(seed: int = 0) -> dict:
    streams_of = jax.random.split(jax.random.key(seed), 6)
    inputs = normal_values(streams_of[0], (BATCH, SEQ_LEN, D), 1.0, 6.0, ((1, 16), (2, 16)))
    cotangent = normal_values(streams_of[1], (BATCH, SEQ_LEN, D), 1.0, 6.0, ((1, 16), (2, 16)))
    kernel = normal_values(streams_of[2], (SEQ_LEN, D), 1.0, 6.0, ((0, 16), (1, 16)))
    factor_one = normal_values(streams_of[3], (BLOCK, BLOCK), BLOCK ** -0.5, 0.375)
    factor_two = normal_values(streams_of[4], (NB, NB), NB ** -0.5, 0.375)
    return dict(inputs=inputs, cotangent=cotangent, kernel=kernel, factor_one=factor_one, factor_two=factor_two)


def to_half(values):
    return lax.optimization_barrier(values.astype(jnp.bfloat16)).astype(jnp.float32)

def reference(inputs, cotangent, kernel, factor_one, factor_two):
    first_factor = factor_one.astype(jnp.float32)
    second_factor = factor_two.astype(jnp.float32)
    kernel_cube = kernel.astype(jnp.float32).reshape(NB, BLOCK, D)

    def sequence(totals, slices):
        grad_first, grad_second, kernel_total = totals
        inputs_seq = slices[0].astype(jnp.float32).reshape(NB, BLOCK, D)
        grads_seq = slices[1].astype(jnp.float32).reshape(NB, BLOCK, D)
        within_mix = to_half(jnp.einsum('cb,abh->ach', first_factor, inputs_seq))
        spectrum = to_half(jnp.einsum('ea,ach->ech', second_factor, within_mix))
        weighted = to_half(kernel_cube * spectrum)
        returned = to_half(jnp.einsum('ea,ech->ach', second_factor, weighted))
        grad_within = to_half(jnp.einsum('cb,abh->ach', first_factor, grads_seq))
        grad_spectrum = to_half(jnp.einsum('ea,ach->ech', second_factor, grad_within))
        grad_weighted = to_half(kernel_cube * grad_spectrum)
        grad_returned = to_half(jnp.einsum('ea,ech->ach', second_factor, grad_weighted))
        grad_seq = jnp.einsum('cb,ach->abh', first_factor, grad_returned).astype(jnp.bfloat16)
        kernel_total = kernel_total + grad_spectrum * spectrum
        grad_first = grad_first + jnp.einsum('ach,abh->cb', returned, grads_seq) + jnp.einsum('ach,abh->cb', grad_returned, inputs_seq)
        grad_second = grad_second + jnp.einsum('ach,ech->ea', grad_within, weighted) + jnp.einsum('ech,ach->ea', grad_weighted, within_mix)
        return ((grad_first, grad_second, kernel_total), grad_seq.reshape(SEQ_LEN, D))
    start = (jnp.zeros((BLOCK, BLOCK), jnp.float32), jnp.zeros((NB, NB), jnp.float32), jnp.zeros((NB, BLOCK, D), jnp.float32))
    totals, grad_inputs = lax.scan(sequence, start, (inputs, cotangent))
    grad_first, grad_second, kernel_total = totals
    scale_first = 1.0 / math.sqrt(BATCH * NB * D)
    scale_second = 1.0 / math.sqrt(BATCH * BLOCK * D)
    grad_kernel = kernel_total.reshape(SEQ_LEN, D).astype(jnp.bfloat16)
    return (grad_inputs, grad_kernel, grad_first * scale_first, grad_second * scale_second)
```

```python
import functools
import math

import jax
import jax.numpy as jnp
from jax import lax
from jax.experimental import pallas as pl
from jax.experimental.pallas import tpu as pltpu
from jax.sharding import PartitionSpec as P

BF16 = jnp.bfloat16
F32 = jnp.float32
NN = (((1,), (0,)), ((), ()))
NT = (((1,), (1,)), ((), ()))
TN = (((0,), (0,)), ((), ()))


def dot(left, right, dims=NN):
    return lax.dot_general(left, right, dims, preferred_element_type=F32)


def put(ref, rows, value):
    ref[0, rows, :] = value[:, 0:128]
    ref[1, rows, :] = value[:, 128:256]


def take(ref, rows):
    return jnp.concatenate([ref[0, rows, :], ref[1, rows, :]], axis=1)


def kernel(
    seq_n, scale_one, scale_two,
    x_hbm, y_hbm, k_hbm, f1_ref, f2_ref,
    gi_hbm, gk_hbm, g1_out, g2_out,
    stage, send, recv, out_send, out_recv, out_stage,
    a_buf, g_buf, k_buf, gk_buf, c_buf, v_buf, f2t_ref,
    gf, red1, acc1, red2, acc2, zbuf, tot, red3, red4,
    load_sem, send_sem, recv_sem, osend_sem, orecv_sem, gsend_sem, grecv_sem, store_sem,
):
    me = lax.axis_index("seq")
    dp = lax.axis_index("dp")
    yc_n = 8
    zh = dp // yc_n
    yc = dp % yc_n
    other_dp = (1 - zh) * yc_n + yc

    def seq_peer(step):
        return lax.rem(me + step, seq_n)

    def yc_peer(step):
        return lax.rem(yc + step, yc_n)

    sources = (x_hbm.at[0], y_hbm.at[0], k_hbm, x_hbm.at[1], y_hbm.at[1])
    loads = []
    for at, source in enumerate(sources):
        loads.append(pltpu.make_async_copy(source, stage.at[at], load_sem.at[at]))
        loads[at].start()

    barrier = pltpu.get_barrier_semaphore()

    @pl.loop(1, seq_n)
    def _(step):
        pl.semaphore_signal(barrier, inc=1, device_id={"seq": seq_peer(step)}, device_id_type=pl.DeviceIdType.MESH)

    @pl.loop(1, yc_n)
    def _(step):
        pl.semaphore_signal(barrier, inc=1, device_id={"dp": zh * yc_n + yc_peer(step)}, device_id_type=pl.DeviceIdType.MESH)

    pl.semaphore_signal(barrier, inc=1, device_id={"dp": other_dp}, device_id_type=pl.DeviceIdType.MESH)

    eye_h = (lax.broadcasted_iota(jnp.int32, (128, 128), 0) == lax.broadcasted_iota(jnp.int32, (128, 128), 1)).astype(F32).astype(BF16)
    eye_b = (lax.broadcasted_iota(jnp.int32, (256, 256), 0) == lax.broadcasted_iota(jnp.int32, (256, 256), 1)).astype(F32).astype(BF16)

    def pack(at):
        @pl.loop(0, 8)
        def _(pair):
            base = pl.multiple_of(pair * 512, 512)
            first = dot(eye_h, stage[at, pl.ds(base, 256), :], NT)
            second = dot(eye_h, stage[at, pl.ds(base + 256, 256), :], NT)
            row = pl.multiple_of(pair * 16, 16)
            for group in range(16):
                both = jnp.concatenate([first[group * 8:group * 8 + 8], second[group * 8:group * 8 + 8]], axis=0)
                send[at, group, pl.ds(row, 16), :] = both.astype(BF16)

    def spread(source, target, send_at, recv_at):
        @pl.loop(1, seq_n)
        def _(step):
            peer = seq_peer(step)
            pltpu.make_async_remote_copy(
                src_ref=source.at[peer], dst_ref=target.at[me], send_sem=send_at, recv_sem=recv_at,
                device_id={"seq": peer}, device_id_type=pl.DeviceIdType.MESH,
            ).start()
        pltpu.make_async_copy(source.at[me], target.at[me], recv_at).start()

    def arrived(target, recv_at):
        pltpu.make_async_copy(target, target, recv_at).wait()

    def drained(source, target, send_at):
        part = source.at[pl.ds(0, source.shape[0] - 1)]
        pltpu.make_async_copy(part, target.at[pl.ds(0, source.shape[0] - 1)], send_at).wait()

    f2t_ref[...] = f2_ref[...].astype(F32).T.astype(BF16)
    gf[...] = jnp.zeros_like(gf)
    for at in range(5):
        loads[at].wait()
        pack(at)
        if at == 0:
            pl.semaphore_wait(barrier, seq_n - 1 + yc_n - 1 + 1)
        spread(send.at[at], recv.at[at], send_sem.at[at], recv_sem.at[at])

    def rows_of(ref, at, block):
        return ref[at, pl.ds(block * 2, 2)].reshape(256, 256)

    def compute(batch, x_at, y_at):
        @pl.loop(0, 8)
        def _(block):
            rows = pl.ds(pl.multiple_of(block * 256, 256), 256)
            put(a_buf, rows, dot(rows_of(recv, x_at, block), f1_ref[...], NT))
            put(g_buf, rows, dot(rows_of(recv, y_at, block), f1_ref[...], NT))
            if batch == 0:
                put(k_buf, rows, rows_of(recv, 2, block).astype(F32))

        @pl.loop(0, 8)
        def _(lane):
            rows = pl.ds(lane, 256, stride=8)
            a = take(a_buf, rows).astype(BF16)
            g = take(g_buf, rows).astype(BF16)
            k = take(k_buf, rows)
            s = dot(f2_ref[...], a).astype(BF16).astype(F32)
            h = dot(f2_ref[...], g).astype(BF16).astype(F32)
            z = (k * s).astype(BF16)
            w = (k * h).astype(BF16)
            if batch == 0:
                put(gk_buf, rows, h * s)
            else:
                put(gk_buf, rows, take(gk_buf, rows) + h * s)
            put(c_buf, rows, dot(f2t_ref[...], z))
            put(v_buf, rows, dot(f2t_ref[...], w))
            gf[256:512, :] += dot(z, g, NT) + dot(w, a, NT)

        @pl.loop(0, 8)
        def _(block):
            rows = pl.ds(pl.multiple_of(block * 256, 256), 256)
            c = take(c_buf, rows).astype(BF16)
            v = take(v_buf, rows).astype(BF16)
            out_send[batch, pl.ds(block * 2, 2)] = dot(v, f1_ref[...]).astype(BF16).reshape(2, 128, 256)
            gf[0:256, :] += dot(c, rows_of(recv, y_at, block), TN) + dot(v, rows_of(recv, x_at, block), TN)
            if batch == 1:
                out_send[2, pl.ds(block * 2, 2)] = take(gk_buf, rows).astype(BF16).reshape(2, 128, 256)

    for at in (0, 1, 2):
        arrived(recv.at[at], recv_sem.at[at])
    compute(0, 0, 1)
    spread(out_send.at[0], out_recv.at[0], osend_sem.at[0], orecv_sem.at[0])
    for at in (3, 4):
        arrived(recv.at[at], recv_sem.at[at])
    compute(1, 3, 4)

    @pl.loop(1, yc_n)
    def _(step):
        peer = yc_peer(step)
        pltpu.make_async_remote_copy(
            src_ref=gf.at[pl.ds(pl.multiple_of(peer * 64, 64), 64)], dst_ref=red1.at[yc],
            send_sem=gsend_sem.at[0], recv_sem=grecv_sem.at[0],
            device_id={"dp": zh * yc_n + peer}, device_id_type=pl.DeviceIdType.MESH,
        ).start()
    pltpu.make_async_copy(gf.at[pl.ds(pl.multiple_of(yc * 64, 64), 64)], red1.at[yc], grecv_sem.at[0]).start()
    arrived(red1, grecv_sem.at[0])
    for block in range(8):
        rows = slice(block * 8, block * 8 + 8)
        total = red1[0, rows, :]
        for slot in range(1, yc_n):
            total = total + red1[slot, rows, :]
        acc1[block * 2] = total[:, 0:128]
        acc1[block * 2 + 1] = total[:, 128:256]
    spread(acc1, red2, gsend_sem.at[1], grecv_sem.at[1])
    spread(out_send.at[2], out_recv.at[2], osend_sem.at[2], orecv_sem.at[2])
    spread(out_send.at[1], out_recv.at[1], osend_sem.at[1], orecv_sem.at[1])

    stores = []

    def unpack(at, target):
        @pl.loop(0, 8)
        def _(pair):
            row = pl.multiple_of(pair * 16, 16)
            firsts, seconds = [], []
            for group in range(16):
                both = out_recv[at, group, pl.ds(row, 16), :].astype(F32)
                firsts.append(both[0:8])
                seconds.append(both[8:16])
            base = pl.multiple_of(pair * 512, 512)
            out_stage[at, pl.ds(base, 256), :] = dot(eye_b, jnp.concatenate(firsts, axis=0).astype(BF16), NT).astype(BF16)
            out_stage[at, pl.ds(base + 256, 256), :] = dot(eye_b, jnp.concatenate(seconds, axis=0).astype(BF16), NT).astype(BF16)
        copy = pltpu.make_async_copy(out_stage.at[at], target, store_sem.at[at])
        copy.start()
        stores.append(copy)

    arrived(out_recv.at[0], orecv_sem.at[0])
    unpack(0, gi_hbm.at[0])

    arrived(red2, grecv_sem.at[1])
    total = red2[0]
    for slot in range(1, 16):
        total = total + red2[slot]
    acc2[...] = total
    across = pltpu.make_async_remote_copy(
        src_ref=acc2, dst_ref=zbuf, send_sem=gsend_sem.at[2], recv_sem=grecv_sem.at[2],
        device_id={"dp": other_dp}, device_id_type=pl.DeviceIdType.MESH,
    )
    across.start()
    across.wait()
    tot[...] = acc2[...] + zbuf[...]

    @pl.loop(1, seq_n)
    def _(step):
        pltpu.make_async_remote_copy(
            src_ref=tot, dst_ref=red3.at[me], send_sem=gsend_sem.at[3], recv_sem=grecv_sem.at[3],
            device_id={"seq": seq_peer(step)}, device_id_type=pl.DeviceIdType.MESH,
        ).start()
    pltpu.make_async_copy(tot, red3.at[me], grecv_sem.at[3]).start()
    arrived(red3, grecv_sem.at[3])

    @pl.loop(1, yc_n)
    def _(step):
        pltpu.make_async_remote_copy(
            src_ref=red3, dst_ref=red4.at[yc], send_sem=gsend_sem.at[4], recv_sem=grecv_sem.at[4],
            device_id={"dp": zh * yc_n + yc_peer(step)}, device_id_type=pl.DeviceIdType.MESH,
        ).start()
    pltpu.make_async_copy(red3, red4.at[yc], grecv_sem.at[4]).start()

    arrived(out_recv.at[2], orecv_sem.at[2])
    unpack(2, gk_hbm)
    arrived(red4, grecv_sem.at[4])
    for slot in range(yc_n):
        for block in range(8):
            out, scale = (g1_out, scale_one) if slot < 4 else (g2_out, scale_two)
            rows = slice((slot % 4) * 64 + block * 8, (slot % 4) * 64 + block * 8 + 8)
            out[rows, 0:128] = red4[slot, block * 2] * scale
            out[rows, 128:256] = red4[slot, block * 2 + 1] * scale
    arrived(out_recv.at[1], orecv_sem.at[1])
    unpack(1, gi_hbm.at[1])

    for at in range(5):
        drained(send.at[at], recv.at[at], send_sem.at[at])
    for at in range(3):
        drained(out_send.at[at], out_recv.at[at], osend_sem.at[at])
    drained(red1, red1, gsend_sem.at[0])
    drained(red2, red2, gsend_sem.at[1])
    drained(red3, red3, gsend_sem.at[3])
    drained(red4, red4, gsend_sem.at[4])
    for copy in stores:
        copy.wait()


def on_device(mesh, inputs, cotangent, kernel_rows, factor_one, factor_two):
    seq_n = mesh.shape["seq"]
    width = mesh.shape["dp"] * inputs.shape[2]
    batch = inputs.shape[0]
    scale_one = 1.0 / math.sqrt(batch * factor_two.shape[0] * width)
    scale_two = 1.0 / math.sqrt(batch * factor_one.shape[0] * width)
    anywhere = pl.BlockSpec(memory_space=pl.ANY)
    vmem = pl.BlockSpec(memory_space=pltpu.VMEM)
    square = pltpu.VMEM((2, 2048, 128), F32)
    return pl.pallas_call(
        functools.partial(kernel, seq_n, scale_one, scale_two),
        out_shape=(
            jax.ShapeDtypeStruct(inputs.shape, BF16),
            jax.ShapeDtypeStruct(kernel_rows.shape, BF16),
            jax.ShapeDtypeStruct((256, 256), F32),
            jax.ShapeDtypeStruct((256, 256), F32),
        ),
        in_specs=[anywhere, anywhere, anywhere, vmem, vmem],
        out_specs=(anywhere, anywhere, vmem, vmem),
        scratch_shapes=[
            pltpu.VMEM((5, 4096, 128), BF16),
            pltpu.VMEM((5, 16, 128, 256), BF16),
            pltpu.VMEM((5, 16, 128, 256), BF16),
            pltpu.VMEM((3, 16, 128, 256), BF16),
            pltpu.VMEM((3, 16, 128, 256), BF16),
            pltpu.VMEM((3, 4096, 128), BF16),
            square, square, square, square, square, square,
            pltpu.VMEM((256, 256), BF16),
            pltpu.VMEM((512, 256), F32),
            pltpu.VMEM((8, 64, 256), F32),
            pltpu.VMEM((16, 8, 128), F32),
            pltpu.VMEM((16, 8, 128), F32),
            pltpu.VMEM((8, 128), F32),
            pltpu.VMEM((8, 128), F32),
            pltpu.VMEM((8, 128), F32),
            pltpu.VMEM((16, 8, 128), F32),
            pltpu.VMEM((8, 16, 8, 128), F32),
            pltpu.SemaphoreType.DMA((5,)),
            pltpu.SemaphoreType.DMA((5,)),
            pltpu.SemaphoreType.DMA((5,)),
            pltpu.SemaphoreType.DMA((3,)),
            pltpu.SemaphoreType.DMA((3,)),
            pltpu.SemaphoreType.DMA((5,)),
            pltpu.SemaphoreType.DMA((5,)),
            pltpu.SemaphoreType.DMA((3,)),
        ],
        compiler_params=pltpu.CompilerParams(
            collective_id=0, has_side_effects=True, vmem_limit_bytes=60 * 1024 * 1024
        ),
    )(inputs, cotangent, kernel_rows, factor_one, factor_two)


def solution(mesh):
    return jax.shard_map(
        functools.partial(on_device, mesh),
        mesh=mesh,
        in_specs=(P(None, "seq", "dp"), P(None, "seq", "dp"), P("seq", "dp"), P(), P()),
        out_specs=(P(None, "seq", "dp"), P("seq", "dp"), P(), P()),
        check_vma=False,
    )
```

```python
import functools
import math

import jax
import jax.numpy as jnp
from jax import lax
from jax.experimental import pallas as pl
from jax.experimental.pallas import tpu as pltpu
from jax.sharding import PartitionSpec as P

BF16 = jnp.bfloat16
F32 = jnp.float32
NN = (((1,), (0,)), ((), ()))
NT = (((1,), (1,)), ((), ()))
TN = (((0,), (0,)), ((), ()))


def dot(left, right, dims=NN):
    return lax.dot_general(left, right, dims, preferred_element_type=F32)


def put(ref, rows, value):
    ref[0, rows, :] = value[:, 0:128]
    ref[1, rows, :] = value[:, 128:256]


def take(ref, rows):
    return jnp.concatenate([ref[0, rows, :], ref[1, rows, :]], axis=1)


def kernel(
    seq_n, scale_one, scale_two,
    x_hbm, y_hbm, k_hbm, f1_hbm, f2_hbm,
    gi_hbm, gk_hbm, g1_out, g2_out,
    stage, send, recv, out_send, out_recv,
    a_buf, g_buf, k_buf, gk_buf, c_buf, v_buf, f1_ref, f2_ref, f2t_ref,
    gf, red1, acc1, red2, acc2, zbuf, tot, red3, red4,
    first_sem, load_sem, send_sem, recv_sem, osend_sem, orecv_sem, gsend_sem, grecv_sem, entered,
):
    me = lax.axis_index("seq")
    dp = lax.axis_index("dp")
    yc_n = 8
    zh = dp // yc_n
    yc = dp % yc_n
    other_dp = (1 - zh) * yc_n + yc

    def seq_peer(step):
        return lax.rem(me + step, seq_n)

    def yc_peer(step):
        return lax.rem(yc + step, yc_n)

    sources = (x_hbm.at[0], y_hbm.at[0], k_hbm, x_hbm.at[1], y_hbm.at[1])
    first_loads = []
    for quarter in range(4):
        rows = pl.ds(quarter * 1024, 1024)
        first_loads.append(pltpu.make_async_copy(sources[0].at[rows], stage.at[0, rows], first_sem.at[quarter]))
    loads = [None]
    for at in range(1, 5):
        loads.append(pltpu.make_async_copy(sources[at], stage.at[at], load_sem.at[at]))
    factor_loads = (
        pltpu.make_async_copy(f1_hbm, f1_ref, load_sem.at[0]),
        pltpu.make_async_copy(f2_hbm, f2_ref, load_sem.at[5]),
    )
    for copy in (*first_loads, *loads[1:], *factor_loads):
        copy.start()

    barrier = pltpu.get_barrier_semaphore()

    @pl.loop(1, seq_n)
    def _(step):
        pl.semaphore_signal(barrier, inc=1, device_id={"seq": seq_peer(step)}, device_id_type=pl.DeviceIdType.MESH)

    @pl.loop(1, yc_n)
    def _(step):
        pl.semaphore_signal(barrier, inc=1, device_id={"dp": zh * yc_n + yc_peer(step)}, device_id_type=pl.DeviceIdType.MESH)

    @pl.when(zh == 0)
    def _():
        pl.semaphore_signal(barrier, inc=1, device_id={"dp": other_dp}, device_id_type=pl.DeviceIdType.MESH)

    eye_h = (lax.broadcasted_iota(jnp.int32, (128, 128), 0) == lax.broadcasted_iota(jnp.int32, (128, 128), 1)).astype(F32).astype(BF16)
    eye_b = (lax.broadcasted_iota(jnp.int32, (256, 256), 0) == lax.broadcasted_iota(jnp.int32, (256, 256), 1)).astype(F32).astype(BF16)

    def pack(at, low, high):
        @pl.loop(low, high)
        def _(pair):
            base = pl.multiple_of(pair * 512, 512)
            first = dot(eye_h, stage[at, pl.ds(base, 256), :], NT)
            second = dot(eye_h, stage[at, pl.ds(base + 256, 256), :], NT)
            row = pl.multiple_of(pair * 16, 16)
            for group in range(16):
                both = jnp.concatenate([first[group * 8:group * 8 + 8], second[group * 8:group * 8 + 8]], axis=0)
                send[at, group, pl.ds(row, 16), :] = both.astype(BF16)

    def spread(source, target, send_at, recv_at):
        @pl.loop(1, seq_n)
        def _(step):
            peer = seq_peer(step)
            pltpu.make_async_remote_copy(
                src_ref=source.at[peer], dst_ref=target.at[me], send_sem=send_at, recv_sem=recv_at,
                device_id={"seq": peer}, device_id_type=pl.DeviceIdType.MESH,
            ).start()
        pltpu.make_async_copy(source.at[me], target.at[me], recv_at).start()

    def spread_quarter(at, quarter):
        rows = pl.ds(quarter * 32, 32)

        @pl.loop(1, seq_n)
        def _(step):
            peer = seq_peer(step)
            pltpu.make_async_remote_copy(
                src_ref=out_send.at[at, peer, rows], dst_ref=out_recv.at[at, me, rows],
                send_sem=osend_sem.at[at, quarter], recv_sem=orecv_sem.at[at, quarter],
                device_id={"seq": peer}, device_id_type=pl.DeviceIdType.MESH,
            ).start()
        pltpu.make_async_copy(out_send.at[at, me, rows], out_recv.at[at, me, rows], orecv_sem.at[at, quarter]).start()

    def quarter_arrived(at, quarter):
        whole = out_recv.at[at, :, pl.ds(quarter * 32, 32)]
        pltpu.make_async_copy(whole, whole, orecv_sem.at[at, quarter]).wait()

    def quarter_drained(at, quarter):
        rows = pl.ds(quarter * 32, 32)
        pltpu.make_async_copy(
            out_send.at[at, pl.ds(0, seq_n - 1), rows], out_recv.at[at, pl.ds(0, seq_n - 1), rows], osend_sem.at[at, quarter]
        ).wait()

    def arrived(target, recv_at):
        pltpu.make_async_copy(target, target, recv_at).wait()

    def drained(source, target, send_at):
        part = source.at[pl.ds(0, source.shape[0] - 1)]
        pltpu.make_async_copy(part, target.at[pl.ds(0, source.shape[0] - 1)], send_at).wait()

    for quarter in range(4):
        first_loads[quarter].wait()
        pack(0, quarter * 2, quarter * 2 + 2)
        if quarter == 0:
            pl.semaphore_wait(barrier, seq_n - 1 + yc_n - 1 + zh)
        rows = pl.ds(quarter * 32, 32)

        @pl.loop(1, seq_n)
        def _(step):
            peer = seq_peer(step)
            pltpu.make_async_remote_copy(
                src_ref=send.at[0, peer, rows], dst_ref=recv.at[0, me, rows], send_sem=send_sem.at[0], recv_sem=recv_sem.at[0],
                device_id={"seq": peer}, device_id_type=pl.DeviceIdType.MESH,
            ).start()
        pltpu.make_async_copy(send.at[0, me, rows], recv.at[0, me, rows], recv_sem.at[0]).start()

    @pl.when(zh == 1)
    def _():
        pl.semaphore_signal(entered, inc=1, device_id={"dp": other_dp}, device_id_type=pl.DeviceIdType.MESH)

    for at in range(1, 5):
        loads[at].wait()
        pack(at, 0, 8)
        spread(send.at[at], recv.at[at], send_sem.at[at], recv_sem.at[at])
    for copy in factor_loads:
        copy.wait()
    f2t_ref[...] = f2_ref[...].astype(F32).T.astype(BF16)
    gf[...] = jnp.zeros_like(gf)

    def rows_of(ref, at, block):
        return ref[at, pl.ds(block * 2, 2)].reshape(256, 256)

    def compute(batch, x_at, y_at):
        @pl.loop(0, 8)
        def _(block):
            rows = pl.ds(pl.multiple_of(block * 256, 256), 256)
            put(a_buf, rows, dot(rows_of(recv, x_at, block), f1_ref[...], NT))
            put(g_buf, rows, dot(rows_of(recv, y_at, block), f1_ref[...], NT))
            if batch == 0:
                put(k_buf, rows, rows_of(recv, 2, block).astype(F32))

        @pl.loop(0, 8)
        def _(lane):
            rows = pl.ds(lane, 256, stride=8)
            a = take(a_buf, rows).astype(BF16)
            g = take(g_buf, rows).astype(BF16)
            k = take(k_buf, rows)
            s = dot(f2_ref[...], a).astype(BF16).astype(F32)
            h = dot(f2_ref[...], g).astype(BF16).astype(F32)
            z = (k * s).astype(BF16)
            w = (k * h).astype(BF16)
            if batch == 0:
                put(gk_buf, rows, h * s)
            else:
                put(gk_buf, rows, take(gk_buf, rows) + h * s)
            put(c_buf, rows, dot(f2t_ref[...], z))
            put(v_buf, rows, dot(f2t_ref[...], w))
            gf[256:512, :] += dot(z, g, NT) + dot(w, a, NT)

        @pl.loop(0, 8)
        def _(block):
            rows = pl.ds(pl.multiple_of(block * 256, 256), 256)
            c = take(c_buf, rows).astype(BF16)
            v = take(v_buf, rows).astype(BF16)
            out_send[batch, pl.ds(block * 2, 2)] = dot(v, f1_ref[...]).astype(BF16).reshape(2, 128, 256)
            gf[0:256, :] += dot(c, rows_of(recv, y_at, block), TN) + dot(v, rows_of(recv, x_at, block), TN)
            if batch == 1:
                out_send[2, pl.ds(block * 2, 2)] = take(gk_buf, rows).astype(BF16).reshape(2, 128, 256)

    for at in (0, 1, 2):
        arrived(recv.at[at], recv_sem.at[at])
    compute(0, 0, 1)
    for quarter in range(4):
        spread_quarter(0, quarter)
    for at in (3, 4):
        arrived(recv.at[at], recv_sem.at[at])
    compute(1, 3, 4)

    @pl.loop(1, yc_n)
    def _(step):
        peer = yc_peer(step)
        pltpu.make_async_remote_copy(
            src_ref=gf.at[pl.ds(pl.multiple_of(peer * 64, 64), 64)], dst_ref=red1.at[yc],
            send_sem=gsend_sem.at[0], recv_sem=grecv_sem.at[0],
            device_id={"dp": zh * yc_n + peer}, device_id_type=pl.DeviceIdType.MESH,
        ).start()
    pltpu.make_async_copy(gf.at[pl.ds(pl.multiple_of(yc * 64, 64), 64)], red1.at[yc], grecv_sem.at[0]).start()
    spread_quarter(2, 0)
    spread_quarter(2, 1)
    arrived(red1, grecv_sem.at[0])
    for block in range(8):
        rows = slice(block * 8, block * 8 + 8)
        total = red1[0, rows, :]
        for slot in range(1, yc_n):
            total = total + red1[slot, rows, :]
        acc1[block * 2] = total[:, 0:128]
        acc1[block * 2 + 1] = total[:, 128:256]
    spread(acc1, red2, gsend_sem.at[1], grecv_sem.at[1])
    spread_quarter(2, 2)

    def unpack(at, quarter, target):
        quarter_arrived(at, quarter)

        @pl.loop(quarter * 2, quarter * 2 + 2)
        def _(pair):
            row = pl.multiple_of(pair * 16, 16)
            firsts, seconds = [], []
            for group in range(16):
                both = out_recv[at, group, pl.ds(row, 16), :].astype(F32)
                firsts.append(both[0:8])
                seconds.append(both[8:16])
            base = pl.multiple_of(pair * 512, 512)
            target[pl.ds(base, 256), :] = dot(eye_b, jnp.concatenate(firsts, axis=0).astype(BF16), NT).astype(BF16)
            target[pl.ds(base + 256, 256), :] = dot(eye_b, jnp.concatenate(seconds, axis=0).astype(BF16), NT).astype(BF16)

    for quarter in range(4):
        unpack(0, quarter, gi_hbm.at[0])

    arrived(red2, grecv_sem.at[1])
    total = red2[0]
    for slot in range(1, 16):
        total = total + red2[slot]
    acc2[...] = total
    @pl.when(zh == 0)
    def _():
        pl.semaphore_wait(entered, 1)

    across = pltpu.make_async_remote_copy(
        src_ref=acc2, dst_ref=zbuf, send_sem=gsend_sem.at[2], recv_sem=grecv_sem.at[2],
        device_id={"dp": other_dp}, device_id_type=pl.DeviceIdType.MESH,
    )
    across.start()
    quarter_drained(2, 0)
    spread_quarter(2, 3)
    quarter_drained(2, 1)
    across.wait()
    tot[...] = acc2[...] + zbuf[...]

    @pl.loop(1, seq_n)
    def _(step):
        pltpu.make_async_remote_copy(
            src_ref=tot, dst_ref=red3.at[me], send_sem=gsend_sem.at[3], recv_sem=grecv_sem.at[3],
            device_id={"seq": seq_peer(step)}, device_id_type=pl.DeviceIdType.MESH,
        ).start()
    pltpu.make_async_copy(tot, red3.at[me], grecv_sem.at[3]).start()
    quarter_drained(2, 2)
    spread_quarter(1, 0)
    quarter_drained(2, 3)
    spread_quarter(1, 1)
    arrived(red3, grecv_sem.at[3])

    @pl.loop(1, yc_n)
    def _(step):
        pltpu.make_async_remote_copy(
            src_ref=red3, dst_ref=red4.at[yc], send_sem=gsend_sem.at[4], recv_sem=grecv_sem.at[4],
            device_id={"dp": zh * yc_n + yc_peer(step)}, device_id_type=pl.DeviceIdType.MESH,
        ).start()
    pltpu.make_async_copy(red3, red4.at[yc], grecv_sem.at[4]).start()
    spread_quarter(1, 2)
    spread_quarter(1, 3)

    for quarter in range(4):
        unpack(2, quarter, gk_hbm)
    arrived(red4, grecv_sem.at[4])
    for slot in range(yc_n):
        for block in range(8):
            out, scale = (g1_out, scale_one) if slot < 4 else (g2_out, scale_two)
            rows = slice((slot % 4) * 64 + block * 8, (slot % 4) * 64 + block * 8 + 8)
            out[rows, 0:128] = red4[slot, block * 2] * scale
            out[rows, 128:256] = red4[slot, block * 2 + 1] * scale
    for at in range(5):
        drained(send.at[at], recv.at[at], send_sem.at[at])
    for quarter in range(4):
        quarter_drained(0, quarter)
    drained(red1, red1, gsend_sem.at[0])
    drained(red2, red2, gsend_sem.at[1])
    drained(red3, red3, gsend_sem.at[3])
    drained(red4, red4, gsend_sem.at[4])
    for quarter in range(4):
        unpack(1, quarter, gi_hbm.at[1])
    for quarter in range(4):
        quarter_drained(1, quarter)


def finish(gi, gk, g1, g2, gi_out, gk_out, g1_out, g2_out, sems):
    copies = [
        pltpu.make_async_copy(source, target, sems.at[at])
        for at, (source, target) in enumerate(((gi, gi_out), (gk, gk_out), (g1, g1_out), (g2, g2_out)))
    ]
    for copy in copies:
        copy.start()
    for copy in copies:
        copy.wait()


def on_device(mesh, inputs, cotangent, kernel_rows, factor_one, factor_two):
    seq_n = mesh.shape["seq"]
    width = mesh.shape["dp"] * inputs.shape[2]
    batch = inputs.shape[0]
    scale_one = 1.0 / math.sqrt(batch * factor_two.shape[0] * width)
    scale_two = 1.0 / math.sqrt(batch * factor_one.shape[0] * width)
    anywhere = pl.BlockSpec(memory_space=pl.ANY)
    far = pl.BlockSpec(memory_space=pltpu.MemorySpace.HBM)
    vmem = pl.BlockSpec(memory_space=pltpu.VMEM)
    square = pltpu.VMEM((2, 2048, 128), F32)
    operands = tuple(
        pltpu.with_memory_space_constraint(value, pltpu.MemorySpace.HBM)
        for value in (inputs, cotangent, kernel_rows, factor_one, factor_two)
    )
    results = pl.pallas_call(
        functools.partial(kernel, seq_n, scale_one, scale_two),
        out_shape=(
            jax.ShapeDtypeStruct(inputs.shape, BF16),
            jax.ShapeDtypeStruct(kernel_rows.shape, BF16),
            jax.ShapeDtypeStruct((256, 256), F32),
            jax.ShapeDtypeStruct((256, 256), F32),
        ),
        in_specs=[far] * 5,
        out_specs=(vmem, vmem, vmem, vmem),
        scratch_shapes=[
            pltpu.VMEM((5, 4096, 128), BF16),
            pltpu.VMEM((5, 16, 128, 256), BF16),
            pltpu.VMEM((5, 16, 128, 256), BF16),
            pltpu.VMEM((3, 16, 128, 256), BF16),
            pltpu.VMEM((3, 16, 128, 256), BF16),
            square, square, square, square, square, square,
            pltpu.VMEM((256, 256), BF16),
            pltpu.VMEM((256, 256), BF16),
            pltpu.VMEM((256, 256), BF16),
            pltpu.VMEM((512, 256), F32),
            pltpu.VMEM((8, 64, 256), F32),
            pltpu.VMEM((16, 8, 128), F32),
            pltpu.VMEM((16, 8, 128), F32),
            pltpu.VMEM((8, 128), F32),
            pltpu.VMEM((8, 128), F32),
            pltpu.VMEM((8, 128), F32),
            pltpu.VMEM((16, 8, 128), F32),
            pltpu.VMEM((8, 16, 8, 128), F32),
            pltpu.SemaphoreType.DMA((4,)),
            pltpu.SemaphoreType.DMA((6,)),
            pltpu.SemaphoreType.DMA((5,)),
            pltpu.SemaphoreType.DMA((5,)),
            pltpu.SemaphoreType.DMA((3, 4)),
            pltpu.SemaphoreType.DMA((3, 4)),
            pltpu.SemaphoreType.DMA((5,)),
            pltpu.SemaphoreType.DMA((5,)),
            pltpu.SemaphoreType.REGULAR,
        ],
        compiler_params=pltpu.CompilerParams(
            collective_id=0, has_side_effects=True, vmem_limit_bytes=42 * 1024 * 1024
        ),
    )(*operands)
    return pl.pallas_call(
        finish,
        out_shape=tuple(jax.ShapeDtypeStruct(r.shape, r.dtype) for r in results),
        in_specs=[anywhere] * 4,
        out_specs=(far,) * 4,
        scratch_shapes=[pltpu.SemaphoreType.DMA((4,))],
        compiler_params=pltpu.CompilerParams(vmem_limit_bytes=4 * 1024 * 1024),
    )(*results)


def solution(mesh):
    return jax.shard_map(
        functools.partial(on_device, mesh),
        mesh=mesh,
        in_specs=(P(None, "seq", "dp"), P(None, "seq", "dp"), P("seq", "dp"), P(), P()),
        out_specs=(P(None, "seq", "dp"), P("seq", "dp"), P(), P()),
        check_vma=False,
    )
```

```python
import functools
import math

import jax
import jax.numpy as jnp
from jax import lax
from jax.experimental import pallas as pl
from jax.experimental.pallas import tpu as pltpu
from jax.sharding import PartitionSpec as P

BF16 = jnp.bfloat16
F32 = jnp.float32
NN = (((1,), (0,)), ((), ()))
NT = (((1,), (1,)), ((), ()))
TN = (((0,), (0,)), ((), ()))


def dot(left, right, dims=NN):
    return lax.dot_general(left, right, dims, preferred_element_type=F32)


def put(ref, rows, value):
    ref[0, rows, :] = value[:, 0:128]
    ref[1, rows, :] = value[:, 128:256]


def take(ref, rows):
    return jnp.concatenate([ref[0, rows, :], ref[1, rows, :]], axis=1)


def kernel(
    seq_n, scale_one, scale_two,
    x_hbm, y_hbm, k_hbm, f1_hbm, f2_hbm,
    gi_hbm, gk_hbm, g1_out, g2_out,
    stage, send, recv, out_send, out_recv,
    a_buf, g_buf, k_buf, gk_buf, c_buf, v_buf, f1_ref, f2_ref, f2t_ref,
    gf, red1, acc1, redx, accx, red2, acc2, zbuf, tot, redz, red3, red4,
    first_sem, load_sem, send_sem, recv_sem, osend_sem, orecv_sem, gsend_sem, grecv_sem, entered,
):
    me = lax.axis_index("seq")
    dp = lax.axis_index("dp")
    yc_n = 8
    zh = dp // yc_n
    yc = dp % yc_n
    other_dp = (1 - zh) * yc_n + yc

    x_at = me // 4
    z_at = me % 4

    def seq_peer(step):
        return lax.rem(me + step, seq_n)

    def yc_peer(step):
        return lax.rem(yc + step, yc_n)

    sources = (x_hbm.at[0], y_hbm.at[0], k_hbm, x_hbm.at[1], y_hbm.at[1])
    first_loads = []
    for quarter in range(4):
        rows = pl.ds(quarter * 1024, 1024)
        first_loads.append(pltpu.make_async_copy(sources[0].at[rows], stage.at[0, rows], first_sem.at[quarter]))
    loads = [None]
    for at in range(1, 5):
        loads.append(pltpu.make_async_copy(sources[at], stage.at[at], load_sem.at[at]))
    factor_loads = (
        pltpu.make_async_copy(f1_hbm, f1_ref, load_sem.at[0]),
        pltpu.make_async_copy(f2_hbm, f2_ref, load_sem.at[5]),
    )
    for copy in (*first_loads, *loads[1:], *factor_loads):
        copy.start()

    barrier = pltpu.get_barrier_semaphore()

    @pl.loop(1, seq_n)
    def _(step):
        pl.semaphore_signal(barrier, inc=1, device_id={"seq": seq_peer(step)}, device_id_type=pl.DeviceIdType.MESH)

    @pl.loop(1, yc_n)
    def _(step):
        pl.semaphore_signal(barrier, inc=1, device_id={"dp": zh * yc_n + yc_peer(step)}, device_id_type=pl.DeviceIdType.MESH)

    @pl.when(zh == 0)
    def _():
        pl.semaphore_signal(barrier, inc=1, device_id={"dp": other_dp}, device_id_type=pl.DeviceIdType.MESH)

    eye_h = (lax.broadcasted_iota(jnp.int32, (128, 128), 0) == lax.broadcasted_iota(jnp.int32, (128, 128), 1)).astype(F32).astype(BF16)
    eye_b = (lax.broadcasted_iota(jnp.int32, (256, 256), 0) == lax.broadcasted_iota(jnp.int32, (256, 256), 1)).astype(F32).astype(BF16)

    def pack(at, low, high):
        @pl.loop(low, high)
        def _(pair):
            base = pl.multiple_of(pair * 512, 512)
            first = dot(eye_h, stage[at, pl.ds(base, 256), :], NT)
            second = dot(eye_h, stage[at, pl.ds(base + 256, 256), :], NT)
            row = pl.multiple_of(pair * 16, 16)
            for group in range(16):
                both = jnp.concatenate([first[group * 8:group * 8 + 8], second[group * 8:group * 8 + 8]], axis=0)
                send[at, group, pl.ds(row, 16), :] = both.astype(BF16)

    def spread(source, target, send_at, recv_at):
        @pl.loop(1, seq_n)
        def _(step):
            peer = seq_peer(step)
            pltpu.make_async_remote_copy(
                src_ref=source.at[peer], dst_ref=target.at[me], send_sem=send_at, recv_sem=recv_at,
                device_id={"seq": peer}, device_id_type=pl.DeviceIdType.MESH,
            ).start()
        pltpu.make_async_copy(source.at[me], target.at[me], recv_at).start()

    def spread_quarter(at, quarter):
        rows = pl.ds(quarter * 16, 16)

        @pl.loop(1, seq_n)
        def _(step):
            peer = seq_peer(step)
            pltpu.make_async_remote_copy(
                src_ref=out_send.at[at, peer, rows], dst_ref=out_recv.at[at, me, rows],
                send_sem=osend_sem.at[at, quarter], recv_sem=orecv_sem.at[at, quarter],
                device_id={"seq": peer}, device_id_type=pl.DeviceIdType.MESH,
            ).start()
        pltpu.make_async_copy(out_send.at[at, me, rows], out_recv.at[at, me, rows], orecv_sem.at[at, quarter]).start()

    def quarter_arrived(at, quarter):
        whole = out_recv.at[at, :, pl.ds(quarter * 16, 16)]
        pltpu.make_async_copy(whole, whole, orecv_sem.at[at, quarter]).wait()

    def quarter_drained(at, quarter):
        rows = pl.ds(quarter * 16, 16)
        pltpu.make_async_copy(
            out_send.at[at, pl.ds(0, seq_n - 1), rows], out_recv.at[at, pl.ds(0, seq_n - 1), rows], osend_sem.at[at, quarter]
        ).wait()

    def arrived(target, recv_at):
        pltpu.make_async_copy(target, target, recv_at).wait()

    def drained(source, target, send_at):
        part = source.at[pl.ds(0, source.shape[0] - 1)]
        pltpu.make_async_copy(part, target.at[pl.ds(0, source.shape[0] - 1)], send_at).wait()

    for quarter in range(4):
        first_loads[quarter].wait()
        pack(0, quarter * 2, quarter * 2 + 2)
        if quarter == 0:
            pl.semaphore_wait(barrier, seq_n - 1 + yc_n - 1 + zh)
        rows = pl.ds(quarter * 32, 32)

        @pl.loop(1, seq_n)
        def _(step):
            peer = seq_peer(step)
            pltpu.make_async_remote_copy(
                src_ref=send.at[0, peer, rows], dst_ref=recv.at[0, me, rows], send_sem=send_sem.at[0], recv_sem=recv_sem.at[0],
                device_id={"seq": peer}, device_id_type=pl.DeviceIdType.MESH,
            ).start()
        pltpu.make_async_copy(send.at[0, me, rows], recv.at[0, me, rows], recv_sem.at[0]).start()

    @pl.when(zh == 1)
    def _():
        pl.semaphore_signal(entered, inc=1, device_id={"dp": other_dp}, device_id_type=pl.DeviceIdType.MESH)

    for at in range(1, 5):
        loads[at].wait()
        pack(at, 0, 8)
        spread(send.at[at], recv.at[at], send_sem.at[at], recv_sem.at[at])
    for copy in factor_loads:
        copy.wait()
    f2t_ref[...] = f2_ref[...].astype(F32).T.astype(BF16)
    gf[...] = jnp.zeros_like(gf)

    def rows_of(ref, at, block):
        return ref[at, pl.ds(block * 2, 2)].reshape(256, 256)

    def compute(batch, x_at, y_at):
        @pl.loop(0, 8)
        def _(block):
            rows = pl.ds(pl.multiple_of(block * 256, 256), 256)
            put(a_buf, rows, dot(rows_of(recv, x_at, block), f1_ref[...], NT))
            put(g_buf, rows, dot(rows_of(recv, y_at, block), f1_ref[...], NT))
            if batch == 0:
                put(k_buf, rows, rows_of(recv, 2, block).astype(F32))

        @pl.loop(0, 8)
        def _(lane):
            rows = pl.ds(lane, 256, stride=8)
            a = take(a_buf, rows).astype(BF16)
            g = take(g_buf, rows).astype(BF16)
            k = take(k_buf, rows)
            s = dot(f2_ref[...], a).astype(BF16).astype(F32)
            h = dot(f2_ref[...], g).astype(BF16).astype(F32)
            z = (k * s).astype(BF16)
            w = (k * h).astype(BF16)
            if batch == 0:
                put(gk_buf, rows, h * s)
            else:
                put(gk_buf, rows, take(gk_buf, rows) + h * s)
            put(c_buf, rows, dot(f2t_ref[...], z))
            put(v_buf, rows, dot(f2t_ref[...], w))
            gf[256:512, :] += dot(z, g, NT) + dot(w, a, NT)

        @pl.loop(0, 8)
        def _(block):
            rows = pl.ds(pl.multiple_of(block * 256, 256), 256)
            c = take(c_buf, rows).astype(BF16)
            v = take(v_buf, rows).astype(BF16)
            out_send[batch, pl.ds(block * 2, 2)] = dot(v, f1_ref[...]).astype(BF16).reshape(2, 128, 256)
            gf[0:256, :] += dot(c, rows_of(recv, y_at, block), TN) + dot(v, rows_of(recv, x_at, block), TN)
            if batch == 1:
                out_send[2, pl.ds(block * 2, 2)] = take(gk_buf, rows).astype(BF16).reshape(2, 128, 256)

    for at in (0, 1, 2):
        arrived(recv.at[at], recv_sem.at[at])
    compute(0, 0, 1)
    for quarter in range(8):
        spread_quarter(0, quarter)
    for at in (3, 4):
        arrived(recv.at[at], recv_sem.at[at])
    compute(1, 3, 4)

    @pl.loop(1, yc_n)
    def _(step):
        peer = yc_peer(step)
        pltpu.make_async_remote_copy(
            src_ref=gf.at[pl.ds(pl.multiple_of(peer * 64, 64), 64)], dst_ref=red1.at[yc],
            send_sem=gsend_sem.at[0], recv_sem=grecv_sem.at[0],
            device_id={"dp": zh * yc_n + peer}, device_id_type=pl.DeviceIdType.MESH,
        ).start()
    pltpu.make_async_copy(gf.at[pl.ds(pl.multiple_of(yc * 64, 64), 64)], red1.at[yc], grecv_sem.at[0]).start()
    for quarter in range(3):
        spread_quarter(2, quarter)
    arrived(red1, grecv_sem.at[0])
    for block in range(8):
        rows = slice(block * 8, block * 8 + 8)
        total = red1[0, rows, :]
        for slot in range(1, yc_n):
            total = total + red1[slot, rows, :]
        acc1[block * 2] = total[:, 0:128]
        acc1[block * 2 + 1] = total[:, 128:256]
    @pl.loop(1, 4)
    def _(step):
        peer = lax.rem(x_at + step, 4)
        pltpu.make_async_remote_copy(
            src_ref=acc1.at[pl.ds(peer * 4, 4)], dst_ref=redx.at[x_at], send_sem=gsend_sem.at[1], recv_sem=grecv_sem.at[1],
            device_id={"seq": peer * 4 + z_at}, device_id_type=pl.DeviceIdType.MESH,
        ).start()
    pltpu.make_async_copy(acc1.at[pl.ds(x_at * 4, 4)], redx.at[x_at], grecv_sem.at[1]).start()
    spread_quarter(2, 3)
    spread_quarter(2, 4)
    arrived(redx, grecv_sem.at[1])
    accx[...] = redx[0] + redx[1] + redx[2] + redx[3]

    @pl.loop(1, 4)
    def _(step):
        peer = lax.rem(z_at + step, 4)
        pltpu.make_async_remote_copy(
            src_ref=accx.at[peer], dst_ref=red2.at[z_at], send_sem=gsend_sem.at[5], recv_sem=grecv_sem.at[5],
            device_id={"seq": x_at * 4 + peer}, device_id_type=pl.DeviceIdType.MESH,
        ).start()
    pltpu.make_async_copy(accx.at[z_at], red2.at[z_at], grecv_sem.at[5]).start()
    spread_quarter(2, 5)

    def unpack(at, quarter, target):
        quarter_arrived(at, quarter)

        @pl.loop(quarter, quarter + 1)
        def _(pair):
            row = pl.multiple_of(pair * 16, 16)
            firsts, seconds = [], []
            for group in range(16):
                both = out_recv[at, group, pl.ds(row, 16), :].astype(F32)
                firsts.append(both[0:8])
                seconds.append(both[8:16])
            base = pl.multiple_of(pair * 512, 512)
            target[pl.ds(base, 256), :] = dot(eye_b, jnp.concatenate(firsts, axis=0).astype(BF16), NT).astype(BF16)
            target[pl.ds(base + 256, 256), :] = dot(eye_b, jnp.concatenate(seconds, axis=0).astype(BF16), NT).astype(BF16)

    for quarter in range(8):
        unpack(0, quarter, gi_hbm.at[0])

    arrived(red2, grecv_sem.at[5])
    total = red2[0]
    for slot in range(1, 4):
        total = total + red2[slot]
    acc2[...] = total
    @pl.when(zh == 0)
    def _():
        pl.semaphore_wait(entered, 1)

    across = pltpu.make_async_remote_copy(
        src_ref=acc2, dst_ref=zbuf, send_sem=gsend_sem.at[2], recv_sem=grecv_sem.at[2],
        device_id={"dp": other_dp}, device_id_type=pl.DeviceIdType.MESH,
    )
    across.start()
    spread_quarter(2, 6)
    spread_quarter(2, 7)
    across.wait()
    tot[...] = acc2[...] + zbuf[...]

    @pl.loop(1, 4)
    def _(step):
        peer = lax.rem(z_at + step, 4)
        pltpu.make_async_remote_copy(
            src_ref=tot, dst_ref=redz.at[z_at], send_sem=gsend_sem.at[6], recv_sem=grecv_sem.at[6],
            device_id={"seq": x_at * 4 + peer}, device_id_type=pl.DeviceIdType.MESH,
        ).start()
    pltpu.make_async_copy(tot, redz.at[z_at], grecv_sem.at[6]).start()
    spread_quarter(1, 0)
    spread_quarter(1, 1)
    arrived(redz, grecv_sem.at[6])

    @pl.loop(1, 4)
    def _(step):
        peer = lax.rem(x_at + step, 4)
        pltpu.make_async_remote_copy(
            src_ref=redz, dst_ref=red3.at[x_at], send_sem=gsend_sem.at[3], recv_sem=grecv_sem.at[3],
            device_id={"seq": peer * 4 + z_at}, device_id_type=pl.DeviceIdType.MESH,
        ).start()
    pltpu.make_async_copy(redz, red3.at[x_at], grecv_sem.at[3]).start()
    spread_quarter(1, 2)
    arrived(red3, grecv_sem.at[3])

    @pl.loop(1, yc_n)
    def _(step):
        pltpu.make_async_remote_copy(
            src_ref=red3, dst_ref=red4.at[yc], send_sem=gsend_sem.at[4], recv_sem=grecv_sem.at[4],
            device_id={"dp": zh * yc_n + yc_peer(step)}, device_id_type=pl.DeviceIdType.MESH,
        ).start()
    pltpu.make_async_copy(red3, red4.at[yc], grecv_sem.at[4]).start()
    for quarter in range(3, 8):
        spread_quarter(1, quarter)

    for quarter in range(8):
        unpack(2, quarter, gk_hbm)
    arrived(red4, grecv_sem.at[4])
    for slot in range(yc_n):
        for block in range(8):
            out, scale = (g1_out, scale_one) if slot < 4 else (g2_out, scale_two)
            rows = slice((slot % 4) * 64 + block * 8, (slot % 4) * 64 + block * 8 + 8)
            out[rows, 0:128] = red4[slot, (block * 2) // 4, (block * 2) % 4] * scale
            out[rows, 128:256] = red4[slot, (block * 2 + 1) // 4, (block * 2 + 1) % 4] * scale
    for at in range(5):
        drained(send.at[at], recv.at[at], send_sem.at[at])
    for quarter in range(8):
        quarter_drained(0, quarter)
        quarter_drained(2, quarter)
    drained(red1, red1, gsend_sem.at[0])
    drained(redx, redx, gsend_sem.at[1])
    drained(red2, red2, gsend_sem.at[5])
    drained(redz, redz, gsend_sem.at[6])
    drained(red3, red3, gsend_sem.at[3])
    drained(red4, red4, gsend_sem.at[4])
    for quarter in range(8):
        unpack(1, quarter, gi_hbm.at[1])
    for quarter in range(8):
        quarter_drained(1, quarter)


def finish(gi, gk, g1, g2, gi_out, gk_out, g1_out, g2_out, sems):
    copies = [
        pltpu.make_async_copy(source, target, sems.at[at])
        for at, (source, target) in enumerate(((gi, gi_out), (gk, gk_out), (g1, g1_out), (g2, g2_out)))
    ]
    for copy in copies:
        copy.start()
    for copy in copies:
        copy.wait()


def on_device(mesh, inputs, cotangent, kernel_rows, factor_one, factor_two):
    seq_n = mesh.shape["seq"]
    width = mesh.shape["dp"] * inputs.shape[2]
    batch = inputs.shape[0]
    scale_one = 1.0 / math.sqrt(batch * factor_two.shape[0] * width)
    scale_two = 1.0 / math.sqrt(batch * factor_one.shape[0] * width)
    anywhere = pl.BlockSpec(memory_space=pl.ANY)
    far = pl.BlockSpec(memory_space=pltpu.MemorySpace.HBM)
    vmem = pl.BlockSpec(memory_space=pltpu.VMEM)
    square = pltpu.VMEM((2, 2048, 128), F32)
    operands = tuple(
        pltpu.with_memory_space_constraint(value, pltpu.MemorySpace.HBM)
        for value in (inputs, cotangent, kernel_rows, factor_one, factor_two)
    )
    results = pl.pallas_call(
        functools.partial(kernel, seq_n, scale_one, scale_two),
        out_shape=(
            jax.ShapeDtypeStruct(inputs.shape, BF16),
            jax.ShapeDtypeStruct(kernel_rows.shape, BF16),
            jax.ShapeDtypeStruct((256, 256), F32),
            jax.ShapeDtypeStruct((256, 256), F32),
        ),
        in_specs=[far] * 5,
        out_specs=(vmem, vmem, vmem, vmem),
        scratch_shapes=[
            pltpu.VMEM((5, 4096, 128), BF16),
            pltpu.VMEM((5, 16, 128, 256), BF16),
            pltpu.VMEM((5, 16, 128, 256), BF16),
            pltpu.VMEM((3, 16, 128, 256), BF16),
            pltpu.VMEM((3, 16, 128, 256), BF16),
            square, square, square, square, square, square,
            pltpu.VMEM((256, 256), BF16),
            pltpu.VMEM((256, 256), BF16),
            pltpu.VMEM((256, 256), BF16),
            pltpu.VMEM((512, 256), F32),
            pltpu.VMEM((8, 64, 256), F32),
            pltpu.VMEM((16, 8, 128), F32),
            pltpu.VMEM((4, 4, 8, 128), F32),
            pltpu.VMEM((4, 8, 128), F32),
            pltpu.VMEM((4, 8, 128), F32),
            pltpu.VMEM((8, 128), F32),
            pltpu.VMEM((8, 128), F32),
            pltpu.VMEM((8, 128), F32),
            pltpu.VMEM((4, 8, 128), F32),
            pltpu.VMEM((4, 4, 8, 128), F32),
            pltpu.VMEM((8, 4, 4, 8, 128), F32),
            pltpu.SemaphoreType.DMA((4,)),
            pltpu.SemaphoreType.DMA((6,)),
            pltpu.SemaphoreType.DMA((5,)),
            pltpu.SemaphoreType.DMA((5,)),
            pltpu.SemaphoreType.DMA((3, 8)),
            pltpu.SemaphoreType.DMA((3, 8)),
            pltpu.SemaphoreType.DMA((7,)),
            pltpu.SemaphoreType.DMA((7,)),
            pltpu.SemaphoreType.REGULAR,
        ],
        compiler_params=pltpu.CompilerParams(
            collective_id=0, has_side_effects=True, vmem_limit_bytes=42 * 1024 * 1024
        ),
    )(*operands)
    return pl.pallas_call(
        finish,
        out_shape=tuple(jax.ShapeDtypeStruct(r.shape, r.dtype) for r in results),
        in_specs=[anywhere] * 4,
        out_specs=(far,) * 4,
        scratch_shapes=[pltpu.SemaphoreType.DMA((4,))],
        compiler_params=pltpu.CompilerParams(vmem_limit_bytes=4 * 1024 * 1024),
    )(*results)


def solution(mesh):
    return jax.shard_map(
        functools.partial(on_device, mesh),
        mesh=mesh,
        in_specs=(P(None, "seq", "dp"), P(None, "seq", "dp"), P("seq", "dp"), P(), P()),
        out_specs=(P(None, "seq", "dp"), P("seq", "dp"), P(), P()),
        check_vma=False,
    )
```
